32 devices in a mesh: lon: 8 (over y, x, core), lat: 4 (over z).
Axes of the slice: x: 2, y: 2, z: 4, core: 2. Of those that a mesh axis runs over, the one named last changes fastest.
Arguments:
- background: float32 [69, 64, 1024], P(None, 'lon', 'lat'), may hold values from -6 to 6
- encoder_weight: bfloat16 [128, 69], replicated, may hold values from -0.75 to 0.75
- convolution_weight: bfloat16 [4, 9, 128, 128], replicated, may hold values from -0.1875 to 0.1875
- decoder_weight: bfloat16 [69, 128], replicated, may hold values from -0.5 to 0.5
- dilations: int32 [4], replicated, may hold values from 1 to 4, as said below
- obs_values: float32 [69, 16384], P(None, ('lon', 'lat')), may hold values from -6 to 6
- obs_prec: float32 [16384], P(('lon', 'lat')), may hold values from 0.25 to 4
- obs_frac: float32 [2, 16384], P(None, ('lon', 'lat')), may hold values from 0 to 1
- obs_dest: int32 [16384, 1], P(('lon', 'lat')), may hold values from 0 to 31; in each aligned block of 512 rows (0 to 511, 512 to 1023, ...) at most 32 rows name the same one
- obs_cell: int32 [16384], P(('lon', 'lat')), may hold values from 0 to 1784
- obs_count: int32 [32], P(('lon', 'lat')), may hold values from 256 to 512, as said below
Outputs:
- analysis: float32 [69, 64, 1024], P(None, 'lon', 'lat')
- innovations: float32 [69, 16384], P(None, ('lon', 'lat'))
The draws below stay inside these ranges and needn't reach their ends.
Inputs may be any that keep to these rules, and one draw needn't show every extreme that they name: `dilations`: every layer's dilation lies in 1 to 4, and some layer has dilation 4. `obs_dest`: devices are numbered 4 * lon index + lat index. Among the 512 rows of one device no owner is named more than 32 times, a bound that some block reaches. `obs_cell`: the code c places the lower stencil corner at local longitude c // 255 and local latitude c % (255) of the owner's block, so all four stencil cells lie in that block. `obs_count`: some device has all 512 rows live.
All inputs are finite; a program needn't handle non-finite values.
Results may differ from the reference program's by a relative error of at most 0.023.
Values may be sent and summed in bfloat16 or wider, within the bound.
A program may use at most 128 MiB of HBM per device.

```python
import math
import jax
import jax.numpy as jnp
import numpy as np
from jax import lax

VARS = 69
C = 128
DMAX = 4
LAYERS = 4
ITERS = 2
CLON = 8
CLAT = 256
OBS_DEV = 512
NLON = 64
NLAT = 1024
NOBS = 16384
N_LAT = 4
DEVICES = 32


def draw_dilations(key, part):
    values = jax.random.randint(jax.random.fold_in(key, 11), (LAYERS,), 1, DMAX + 1).astype(jnp.int32)
    position = jax.random.randint(jax.random.fold_in(key, 12), (), 0, LAYERS)
    return values.at[position].set(DMAX)


def draw_obs_count(key, part):
    values = jax.random.randint(jax.random.fold_in(key, 21), (DEVICES,), OBS_DEV // 2, OBS_DEV + 1).astype(jnp.int32)
    position = jax.random.randint(jax.random.fold_in(key, 22), (), 0, DEVICES)
    return values.at[position].set(OBS_DEV)


def place_ends(array, key, smallest, top_value):
    longest = array.shape.index(max(array.shape))
    spots = []
    for shift in (0, 1):
        where = [jax.random.randint(jax.random.fold_in(key, axis), (), 0, length) for axis, length in enumerate(array.shape)]
        where[longest] = (where[longest] + shift) % array.shape[longest]
        spots.append(tuple(where))
    return array.at[spots[0]].set(smallest).at[spots[1]].set(top_value)


def level_of(key, shape, pieces, smallest, high):
    def one(dim, shards_of):
        draws = jax.random.uniform(jax.random.fold_in(jax.random.fold_in(key, 6), dim), (shards_of,), jnp.float32, smallest / len(pieces), high / len(pieces))
        return jnp.repeat(jnp.exp(draws), shape[dim] // shards_of).reshape((-1,) + (1,) * (len(shape) - dim - 1))

    gain = one(*pieces[0])
    for cut in pieces[1:]:
        gain = gain * one(*cut)
    return gain


def routed_block(rng, own, number, rows, count, top, bound, lean):
    order = jax.random.permutation(rng, count)
    crowded, common = load_shares(count, rows * top, bound, lean, True), load_shares(count, rows * top, bound, lean, False)
    places = jnp.arange(count)

    def named(sizes, turn):
        used = int((sizes > 0).sum())
        fixed = max(1, used // 4)
        moved = fixed + (places - fixed + turn * (used - fixed)) % max(1, count - fixed)
        return jnp.zeros((count,), jnp.int32).at[order[jnp.where(places < fixed, places, moved)]].set(jnp.asarray(sizes, jnp.int32))

    sizes = jnp.where(number % 4 == 0, named(crowded, number // 4), named(common, number - number // 4 - 1))
    mixed = jax.random.permutation(jax.random.fold_in(own, 3), count)
    giver, receiver = mixed[0:count // 2 * 2:2], mixed[1:count // 2 * 2:2]
    slack = jnp.minimum(sizes[giver] - 1, bound - sizes[receiver]) // 2
    slack = jnp.where((giver == order[0]) | (receiver == order[0]) | (sizes[receiver] == 0), 0, jnp.maximum(slack, 0))
    moved = jax.random.randint(jax.random.fold_in(own, 4), (count // 2,), 0, 1 << 20) % (slack + 1)
    sizes = sizes.at[giver].add(-moved).at[receiver].add(moved)
    members = jnp.searchsorted(jnp.cumsum(sizes), jnp.arange(rows * top), side="right").astype(jnp.int32)
    listing = members.reshape(top, rows).T
    listing = listing[jax.random.permutation(jax.random.fold_in(own, 1), rows)]
    turn = jax.random.randint(jax.random.fold_in(own, 2), (rows, 1), 0, top)
    return jnp.take_along_axis(listing, (jnp.arange(top)[None, :] + turn) % top, axis=1)


def load_shares(amount, total, limit, slope, full):
    weights = [(1 << 20) // math.isqrt(rank ** slope) + 1 for rank in range(1, amount + 1)]
    largest = limit if full else min(limit, max(-(-total // amount), total * weights[0] // sum(weights)))
    least = 1 if total - largest >= amount - 1 else 0
    given, surplus = [largest] + [least] * (amount - 1), total - largest - least * (amount - 1)
    while surplus > 0:
        candidates = [i for i in range(1, amount) if given[i] < largest] or [i for i in range(1, amount) if given[i] < limit]
        pool, remaining = sum([weights[i] for i in candidates]), surplus
        for i in candidates:
            more = min(limit - given[i], max(1, remaining * weights[i] // pool), surplus)
            given[i] = given[i] + more
            surplus = surplus - more
    return np.array(given)


def normal_values(key, shape, scale, reach, split=(), kind=jnp.bfloat16):
    gain = level_of(key, shape, split, -0.22, 0.18) if split else 1.0
    result = jax.random.normal(key, shape, jnp.float32) * scale * gain
    return jnp.minimum(jnp.maximum(result, -reach), reach).astype(kind)


def setup_inputs(seed: int = 0) -> dict:
    splits = jax.random.split(jax.random.key(seed), 12)
    background = normal_values(splits[0], (VARS, NLON, NLAT), 1.0, 6.0, ((1, 8), (2, 4)), jnp.float32)
    encoder_weight = normal_values(splits[1], (C, VARS), VARS ** -0.5, 0.75)
    convolution_weight = normal_values(splits[2], (LAYERS, 9, C, C), (9 * C) ** -0.5, 0.1875)
    decoder_weight = normal_values(splits[3], (VARS, C), C ** -0.5, 0.5)
    dilations = draw_dilations(jax.random.fold_in(splits[11], 71), 0)
    obs_values = normal_values(splits[5], (VARS, NOBS), 1.0, 6.0, ((1, 32),), jnp.float32)
    obs_prec = jnp.clip(jnp.exp(math.log(4.0) - 2.7725887 * jax.random.uniform(splits[6], (NOBS,), jnp.float32) ** level_of(splits[6], (NOBS,), ((0, 32),), -0.2, 0.2)), 0.25, 4.0)
    obs_frac = jnp.clip(1.0 * jax.random.uniform(splits[7], (2, NOBS), jnp.float32) ** level_of(splits[7], (2, NOBS), ((1, 32),), -0.2, 0.2), 0.0, 1.0)
    obs_dest_keys = jax.random.split(jax.random.fold_in(splits[8], 1), NOBS // OBS_DEV)
    obs_dest_turns = jax.random.permutation(jax.random.fold_in(splits[8], 3), NOBS // OBS_DEV)
    obs_dest = jax.vmap(lambda own, number: routed_block(jax.random.fold_in(splits[8], 2), own, number, OBS_DEV, DEVICES, 1, 2 * OBS_DEV // DEVICES, 2))(obs_dest_keys, obs_dest_turns).reshape((NOBS, 1))
    obs_cell = place_ends(jax.random.randint(splits[9], (NOBS,), 0, (CLON - 1) * (CLAT - 1)), jax.random.fold_in(splits[9], 1), 0, ((CLON - 1) * (CLAT - 1)) - 1).astype(jnp.int32)
    obs_count = draw_obs_count(jax.random.fold_in(splits[11], 71), 0)
    return {"background": background, "encoder_weight": encoder_weight, "convolution_weight": convolution_weight, "decoder_weight": decoder_weight, "dilations": dilations, "obs_values": obs_values, "obs_prec": obs_prec, "obs_frac": obs_frac, "obs_dest": obs_dest, "obs_cell": obs_cell, "obs_count": obs_count}


step_size = 0.25


def shifted(field, move_lon, move_lat):
    rolled = jnp.roll(field, -move_lon, axis=1)
    padded = jnp.pad(rolled, ((0, 0), (0, 0), (DMAX, DMAX)))
    return lax.dynamic_slice_in_dim(padded, DMAX + move_lat, NLAT, 2)


def convolve(activity, kernels, dilation, backward):
    summed = jnp.zeros(activity.shape, jnp.float32)
    source = activity.astype(jnp.float32)
    for step_lon in (-1, 0, 1):
        for step_lat in (-1, 0, 1):
            tap_index = 3 * (step_lon + 1) + (step_lat + 1)
            kernel = kernels[tap_index].astype(jnp.float32)
            if backward:
                window = shifted(source, -step_lon * dilation, -step_lat * dilation)
                summed = summed + jnp.einsum("oc,ohw->chw", kernel, window)
            else:
                window = shifted(source, step_lon * dilation, step_lat * dilation)
                summed = summed + jnp.einsum("oc,chw->ohw", kernel, window)
    return summed


def reference(background, encoder_weight, convolution_weight, decoder_weight, dilations, obs_values, obs_prec, obs_frac, obs_dest, obs_cell, obs_count):
    row_index = jnp.arange(NOBS, dtype=jnp.int32)
    holder_of = row_index // OBS_DEV
    live = (row_index % OBS_DEV < obs_count[holder_of]).astype(jnp.float32)
    target = obs_dest[:, 0]
    base_lon = (target // N_LAT) * CLON + obs_cell // (CLAT - 1)
    base_lat = (target % N_LAT) * CLAT + obs_cell % (CLAT - 1)
    frac_lon = obs_frac[0]
    frac_lat = obs_frac[1]
    corners = ((base_lon, base_lat), (base_lon + 1, base_lat), (base_lon, base_lat + 1), (base_lon + 1, base_lat + 1))
    weights = ((1.0 - frac_lon) * (1.0 - frac_lat), frac_lon * (1.0 - frac_lat), (1.0 - frac_lon) * frac_lat, frac_lon * frac_lat)
    field_to_latent_map = encoder_weight.astype(jnp.float32)
    latent_to_field_map = decoder_weight.astype(jnp.float32)
    current_field = background
    innovation = jnp.zeros_like(obs_values)
    for iteration in range(ITERS):
        latent_width = jnp.einsum("cv,vhw->chw", field_to_latent_map, current_field.astype(jnp.bfloat16).astype(jnp.float32))
        field_history = []
        for layer_index in range(LAYERS):
            field_history.append(latent_width)
            activity = jnp.tanh(latent_width).astype(jnp.bfloat16)
            latent_width = latent_width + convolve(activity, convolution_weight[layer_index], dilations[layer_index], False)
        predicted_field = current_field + jnp.einsum("pf,fms->pms", latent_to_field_map, latent_width.astype(jnp.bfloat16).astype(jnp.float32))
        counterpart_of_measurement = jnp.zeros_like(obs_values)
        for lower_left_gridnode, scaling_coefficient in zip(corners, weights):
            counterpart_of_measurement = counterpart_of_measurement + scaling_coefficient[None, :] * predicted_field[:, lower_left_gridnode[0], lower_left_gridnode[1]]
        innovation = live[None, :] * (counterpart_of_measurement - obs_values)
        scaled_departure = obs_prec[None, :] * innovation
        predicted_sensitivity = jnp.zeros_like(predicted_field)
        for lower_left_gridnode, scaling_coefficient in zip(corners, weights):
            predicted_sensitivity = predicted_sensitivity.at[:, lower_left_gridnode[0], lower_left_gridnode[1]].add(scaling_coefficient[None, :] * scaled_departure)
        reverse_sweep_carry = jnp.einsum("hi,heb->ieb", latent_to_field_map, predicted_sensitivity.astype(jnp.bfloat16).astype(jnp.float32))
        for layer_index in reversed(range(LAYERS)):
            adjoint = convolve(reverse_sweep_carry.astype(jnp.bfloat16), convolution_weight[layer_index], dilations[layer_index], True)
            squashed = jnp.tanh(field_history[layer_index])
            reverse_sweep_carry = reverse_sweep_carry + (1.0 - squashed * squashed) * adjoint
        field_sensitivity = predicted_sensitivity + jnp.einsum("bk,bhn->khn", field_to_latent_map, reverse_sweep_carry.astype(jnp.bfloat16).astype(jnp.float32))
        current_field = current_field - step_size * ((current_field - background) + field_sensitivity)
    return current_field, innovation
```

```python
import functools

import jax
import jax.numpy as jnp
from jax import lax
from jax.experimental import pallas as pl
from jax.experimental.pallas import tpu as pltpu
from jax.sharding import PartitionSpec as P

DMAX = 4
ITERS = 2
step_size = 0.25
MESH = pl.DeviceIdType.MESH
NT = (((1,), (1,)), ((), ()))
TN = (((0,), (0,)), ((), ()))
NN = (((1,), (0,)), ((), ()))
LON_PAD = 8


def snake(i):
    return (i // 4) * 4 + ((i // 2 + i // 4) % 2) * 2 + i % 2


def flip(p, z, nl):
    return p + (z % 2) * (nl - 1 - 2 * p)


def sweep_kernel(backward, nl, nz, layers, dil, x_ref, win_ref, conv_ref, wout_ref, *refs):
    if backward:
        (t_ref, out_ref, carry, recv, outs, land, halo, edge, ext, cols,
         in_send, in_recv, h_send, h_recv, o_send, o_recv, own_sem) = refs
    else:
        (out_ref, t_ref, carry, recv, outs, land, halo, edge, ext, cols,
         in_send, in_recv, h_send, h_recv, o_send, o_recv, own_sem) = refs
    rows, nlon, ch = carry.shape
    w = nlon // nl
    width = rows * w
    i = lax.axis_index("lon")
    z = lax.axis_index("lat")
    s = flip(snake(i), z, nl)
    first = s == 0
    last = s == nl - 1
    low_edge = jnp.logical_and(first, z == 0)
    high_edge = jnp.logical_and(last, z == nz - 1)
    down_s = jnp.maximum(s - 1, 0)
    up_s = jnp.minimum(s + 1, nl - 1)
    down_i = jnp.where(first, i, snake(flip(down_s, z, nl)))
    up_i = jnp.where(last, i, snake(flip(up_s, z, nl)))
    down_z = jnp.where(first, jnp.maximum(z - 1, 0), z)
    up_z = jnp.where(last, jnp.minimum(z + 1, nz - 1), z)

    barrier = pltpu.get_barrier_semaphore()
    for k in range(1, nl):
        pl.semaphore_signal(barrier, inc=1, device_id=((i + k) % nl, z), device_id_type=MESH)

    @pl.when(jnp.logical_and(first, z > 0))
    def _():
        pl.semaphore_signal(barrier, inc=1, device_id=(i, down_z), device_id_type=MESH)

    @pl.when(jnp.logical_and(last, z < nz - 1))
    def _():
        pl.semaphore_signal(barrier, inc=1, device_id=(i, up_z), device_id_type=MESH)

    other_bands = (
        jnp.logical_and(first, z > 0).astype(jnp.int32)
        + jnp.logical_and(last, z < nz - 1).astype(jnp.int32)
    )
    pl.semaphore_wait(barrier, nl - 1 + other_bands)

    def chunk(number):
        return pl.ds(pl.multiple_of(number * width, width), width)

    sends = []
    for k in range(1, nl):
        j = (i + k) % nl
        copy = pltpu.make_async_remote_copy(
            src_ref=x_ref.at[:, chunk(flip(snake(j), z, nl))],
            dst_ref=recv.at[:, chunk(i)],
            send_sem=in_send.at[k], recv_sem=in_recv.at[k],
            device_id=(j, z), device_id_type=MESH,
        )
        copy.start()
        sends.append(copy)
    own = pltpu.make_async_copy(x_ref.at[:, chunk(s)], recv.at[:, chunk(i)], own_sem)
    own.start()

    @pl.when(low_edge)
    def _():
        halo[:, 0] = jnp.zeros_like(halo[:, 0])

    @pl.when(high_edge)
    def _():
        halo[:, 1] = jnp.zeros_like(halo[:, 1])

    own.wait()
    for copy in sends:
        copy.wait()
    for j in range(nl):
        block = lax.dot_general(
            recv[:, j * width:(j + 1) * width], win_ref[...], TN,
            preferred_element_type=jnp.float32,
        )
        carry[:, j * w:(j + 1) * w, :] = block.reshape(rows, w, ch)

    def halo_copies(layer):
        up = pltpu.make_async_remote_copy(
            src_ref=edge.at[layer, 1], dst_ref=halo.at[layer, 0],
            send_sem=h_send.at[layer, 0], recv_sem=h_recv.at[layer, 0],
            device_id=(up_i, up_z), device_id_type=MESH,
        )
        down = pltpu.make_async_remote_copy(
            src_ref=edge.at[layer, 0], dst_ref=halo.at[layer, 1],
            send_sem=h_send.at[layer, 1], recv_sem=h_recv.at[layer, 1],
            device_id=(down_i, down_z), device_id_type=MESH,
        )
        return up, down

    def layer_step(step, _):
        layer = layers - 1 - step if backward else step
        d = dil[layer]

        def activity(r0, r1):
            a = carry[r0:r1]
            if backward:
                return a
            a = jnp.tanh(a)
            t_ref[layer, r0:r1] = a
            return a

        def widen(a, r0):
            n = a.shape[0]
            ext[r0:r0 + n, LON_PAD:LON_PAD + nlon, :] = a
            ext[r0:r0 + n, 0:LON_PAD, :] = a[:, nlon - LON_PAD:, :]
            ext[r0:r0 + n, LON_PAD + nlon:, :] = a[:, :LON_PAD, :]

        def columns(r0, r1):
            for b in range(3):
                cols[r0:r1, :, b * ch:(b + 1) * ch] = ext[
                    r0:r1, pl.ds(LON_PAD + (b - 1) * d, nlon), :
                ].astype(jnp.bfloat16)

        def convolved(r0, r1):
            n = r1 - r0
            total = None
            for a in range(3):
                part = lax.dot_general(
                    cols[pl.ds(DMAX + r0 + (a - 1) * d, n)].reshape(n * nlon, 3 * ch),
                    conv_ref[layer, a], NN if backward else NT,
                    preferred_element_type=jnp.float32,
                )
                total = part if total is None else total + part
            total = total.reshape(n, nlon, ch)
            if backward:
                t = t_ref[layer, r0:r1]
                total = (1.0 - t * t) * total
            carry[r0:r1] = carry[r0:r1] + total

        low = activity(0, DMAX)
        high = activity(rows - DMAX, rows)
        edge[layer, 0] = low.astype(jnp.bfloat16)
        edge[layer, 1] = high.astype(jnp.bfloat16)
        up, down = halo_copies(layer)

        @pl.when(jnp.logical_not(high_edge))
        def _():
            up.start()

        @pl.when(jnp.logical_not(low_edge))
        def _():
            down.start()

        widen(low, DMAX)
        widen(high, rows)
        for r0 in range(DMAX, rows - DMAX, 8):
            widen(activity(r0, r0 + 8), DMAX + r0)
        for r0 in range(DMAX, DMAX + rows, 8):
            columns(r0, r0 + 8)
        for r0 in range(DMAX, rows - DMAX, 8):
            convolved(r0, r0 + 8)

        @pl.when(jnp.logical_not(high_edge))
        def _():
            up.wait_send()
            down.wait_recv()

        @pl.when(jnp.logical_not(low_edge))
        def _():
            down.wait_send()
            up.wait_recv()

        widen(halo[layer, 0].astype(jnp.float32), 0)
        widen(halo[layer, 1].astype(jnp.float32), DMAX + rows)
        columns(0, DMAX)
        columns(DMAX + rows, 2 * DMAX + rows)
        convolved(0, DMAX)
        convolved(rows - DMAX, rows)
        return 0

    lax.fori_loop(0, layers, layer_step, 0)

    for j in range(nl):
        block = carry[:, j * w:(j + 1) * w, :].reshape(width, ch).astype(jnp.bfloat16)
        outs[:, j * width:(j + 1) * width] = lax.dot_general(
            wout_ref[...], block, NT, preferred_element_type=jnp.float32
        ).astype(jnp.bfloat16)
    sends = []
    for k in range(1, nl):
        j = (i + k) % nl
        copy = pltpu.make_async_remote_copy(
            src_ref=outs.at[:, chunk(j)], dst_ref=land.at[:, chunk(s)],
            send_sem=o_send.at[k], recv_sem=o_recv.at[k],
            device_id=(j, z), device_id_type=MESH,
        )
        copy.start()
        sends.append(copy)
    own = pltpu.make_async_copy(outs.at[:, chunk(i)], land.at[:, chunk(s)], own_sem)
    own.start()
    own.wait()
    for copy in sends:
        copy.wait()
    out_ref[...] = land[...]


def sweep(backward, nl, nz, dilations, x, w_in, conv, w_out, tanhs, rows, nlon):
    layers, ch = conv.shape[0], w_in.shape[1]
    vars_, cells = x.shape
    bf, f4 = jnp.bfloat16, jnp.float32
    vmem = pl.BlockSpec(memory_space=pltpu.VMEM)
    out_shape = [jax.ShapeDtypeStruct((vars_, cells), bf)]
    if not backward:
        out_shape.append(jax.ShapeDtypeStruct((layers, rows, nlon, ch), f4))
    args = [dilations, x, w_in, conv, w_out] + ([tanhs] if backward else [])
    dma = pltpu.SemaphoreType.DMA
    return pl.pallas_call(
        functools.partial(sweep_kernel, backward, nl, nz, layers),
        out_shape=out_shape,
        in_specs=[pl.BlockSpec(memory_space=pltpu.SMEM)] + [vmem] * (len(args) - 1),
        out_specs=[vmem] * len(out_shape),
        scratch_shapes=[
            pltpu.VMEM((rows, nlon, ch), f4),
            pltpu.VMEM((vars_, cells), bf),
            pltpu.VMEM((vars_, cells), bf),
            pltpu.VMEM((vars_, cells), bf),
            pltpu.VMEM((layers, 2, DMAX, nlon, ch), bf),
            pltpu.VMEM((layers, 2, DMAX, nlon, ch), bf),
            pltpu.VMEM((rows + 2 * DMAX, nlon + 2 * LON_PAD, ch), f4),
            pltpu.VMEM((rows + 2 * DMAX, nlon, 3 * ch), bf),
            dma((nl,)), dma((nl,)), dma((layers, 2)), dma((layers, 2)),
            dma((nl,)), dma((nl,)), dma(()),
        ],
        compiler_params=pltpu.CompilerParams(
            collective_id=1 if backward else 0, has_side_effects=True,
            vmem_limit_bytes=48 << 20,
        ),
    )(*args)


def on_device(background, encoder_weight, convolution_weight, decoder_weight, dilations,
              obs_values, obs_prec, obs_frac, obs_dest, obs_cell, obs_count):
    bf, f4 = jnp.bfloat16, jnp.float32
    nl, nz = lax.axis_size("lon"), lax.axis_size("lat")
    devices = nl * nz
    nvar, clon, clat = background.shape
    cells = clon * clat
    rows, nlon = clat // nl, clon * nl
    nrow = obs_dest.shape[0]
    capacity = 2 * nrow // devices
    total = 2 * nrow
    vpad = -(-nvar // 16) * 16
    layers, _, ch, _ = convolution_weight.shape

    target = obs_dest[:, 0]
    member = (target[:, None] == jnp.arange(devices, dtype=jnp.int32)[None, :]).astype(jnp.int32)
    before = jnp.sum((jnp.cumsum(member, axis=0) - member) * member, axis=1)
    slots = target * capacity + before
    alive = (jnp.arange(nrow, dtype=jnp.int32) < obs_count[0]).astype(f4)
    base = (obs_cell % (clat - 1)) * clon + obs_cell // (clat - 1)
    request = jnp.concatenate(
        [obs_values, (alive * obs_prec)[None], base.astype(f4)[None], obs_frac], axis=0
    )
    request = jnp.zeros((request.shape[0], total), f4).at[:, slots].set(request)
    arrived = lax.all_to_all(request, ("lon", "lat"), split_axis=1, concat_axis=1, tiled=True)
    owned_obs = arrived[:nvar]
    owned_prec = arrived[nvar]
    corner = arrived[nvar + 1].astype(jnp.int32)[:, None]
    u, v = arrived[nvar + 2][:, None], arrived[nvar + 3][:, None]
    place = lax.broadcasted_iota(jnp.int32, (total, cells), 1) - corner
    zero = jnp.zeros((), f4)
    stencil = (
        jnp.where(place == 0, (1.0 - u) * (1.0 - v), zero)
        + jnp.where(place == 1, u * (1.0 - v), zero)
        + jnp.where(place == clon, (1.0 - u) * v, zero)
        + jnp.where(place == clon + 1, u * v, zero)
    ).astype(bf)

    taps = convolution_weight.reshape(layers, 3, 3, ch, ch)
    forward_w = taps.transpose(0, 2, 3, 1, 4).reshape(layers, 3, ch, 3 * ch)
    backward_w = taps[:, ::-1, ::-1].transpose(0, 2, 1, 3, 4).reshape(layers, 3, 3 * ch, ch)
    enc = jnp.pad(encoder_weight.T, ((0, vpad - nvar), (0, 0)))
    dec = jnp.pad(decoder_weight, ((0, vpad - nvar), (0, 0)))

    field0 = background.transpose(0, 2, 1).reshape(nvar, cells)
    field0 = jnp.pad(field0, ((0, vpad - nvar), (0, 0)))
    field = field0
    for iteration in range(ITERS):
        change, tanhs = sweep(
            False, nl, nz, dilations, field.astype(bf), enc, forward_w, dec, None, rows, nlon
        )
        forecast = field + change.astype(f4)
        head = forecast.astype(bf)
        tail = (forecast - head.astype(f4)).astype(bf)
        both = lax.dot_general(
            jnp.concatenate([head, tail], axis=0), stencil, NT, preferred_element_type=f4
        )
        equivalent = (both[:vpad] + both[vpad:])[:nvar]
        weighted = (owned_prec[None, :] * (equivalent - owned_obs)).astype(bf)
        weighted = jnp.pad(weighted, ((0, vpad - nvar), (0, 0)))
        grad = lax.dot_general(weighted, stencil, NN, preferred_element_type=f4)
        if iteration == ITERS - 1:
            returned = lax.all_to_all(
                equivalent.astype(bf), ("lon", "lat"), split_axis=1, concat_axis=1, tiled=True
            )
            innovation = alive[None, :] * (jnp.take(returned, slots, axis=1).astype(f4) - obs_values)
        back, = sweep(
            True, nl, nz, dilations, grad.astype(bf), dec, backward_w, enc, tanhs, rows, nlon
        )
        field = field - step_size * ((field - field0) + (grad + back.astype(f4)))
    analysis = field[:nvar].reshape(nvar, clat, clon).transpose(0, 2, 1)
    return analysis, innovation


def solution(mesh):
    placed = (
        P(None, "lon", "lat"), P(), P(), P(), P(),
        P(None, ("lon", "lat")), P(("lon", "lat")), P(None, ("lon", "lat")),
        P(("lon", "lat"), None), P(("lon", "lat")), P(("lon", "lat")),
    )
    return jax.shard_map(
        on_device, mesh=mesh, in_specs=placed,
        out_specs=(P(None, "lon", "lat"), P(None, ("lon", "lat"))), check_vma=False,
    )
```

```python
import functools

import jax
import jax.numpy as jnp
from jax import lax
from jax.experimental import pallas as pl
from jax.experimental.pallas import tpu as pltpu
from jax.sharding import PartitionSpec as P

DMAX = 4
ITERS = 2
step_size = 0.25
MESH = pl.DeviceIdType.MESH
NT = (((1,), (1,)), ((), ()))
TN = (((0,), (0,)), ((), ()))
NN = (((1,), (0,)), ((), ()))
LON_PAD = 8


def snake(i):
    return (i // 4) * 4 + ((i // 2 + i // 4) % 2) * 2 + i % 2


def flip(p, z, nl):
    return p + (z % 2) * (nl - 1 - 2 * p)


def sweep_kernel(backward, nl, nz, layers, dil, x_ref, win_ref, conv_ref, wout_ref, *refs):
    if backward:
        (t_ref, out_ref, carry, recv, outs, land, halo, edge, ext, cols,
         in_send, in_recv, h_send, h_recv, o_send, o_recv, own_sem) = refs
    else:
        (out_ref, t_ref, carry, recv, outs, land, halo, edge, ext, cols,
         in_send, in_recv, h_send, h_recv, o_send, o_recv, own_sem) = refs
    rows, nlon, ch = carry.shape
    w = nlon // nl
    width = rows * w
    i = lax.axis_index("lon")
    z = lax.axis_index("lat")
    s = flip(snake(i), z, nl)
    first = s == 0
    last = s == nl - 1
    low_edge = jnp.logical_and(first, z == 0)
    high_edge = jnp.logical_and(last, z == nz - 1)
    down_s = jnp.maximum(s - 1, 0)
    up_s = jnp.minimum(s + 1, nl - 1)
    down_i = jnp.where(first, i, snake(flip(down_s, z, nl)))
    up_i = jnp.where(last, i, snake(flip(up_s, z, nl)))
    down_z = jnp.where(first, jnp.maximum(z - 1, 0), z)
    up_z = jnp.where(last, jnp.minimum(z + 1, nz - 1), z)

    barrier = pltpu.get_barrier_semaphore()
    for k in range(1, nl):
        pl.semaphore_signal(barrier, inc=1, device_id=((i + k) % nl, z), device_id_type=MESH)

    @pl.when(jnp.logical_and(first, z > 0))
    def _():
        pl.semaphore_signal(barrier, inc=1, device_id=(i, down_z), device_id_type=MESH)

    @pl.when(jnp.logical_and(last, z < nz - 1))
    def _():
        pl.semaphore_signal(barrier, inc=1, device_id=(i, up_z), device_id_type=MESH)

    other_bands = (
        jnp.logical_and(first, z > 0).astype(jnp.int32)
        + jnp.logical_and(last, z < nz - 1).astype(jnp.int32)
    )
    pl.semaphore_wait(barrier, nl - 1 + other_bands)

    def chunk(number):
        return pl.ds(pl.multiple_of(number * width, width), width)

    sends = []
    for k in range(1, nl):
        j = (i + k) % nl
        copy = pltpu.make_async_remote_copy(
            src_ref=x_ref.at[:, chunk(flip(snake(j), z, nl))],
            dst_ref=recv.at[:, chunk(i)],
            send_sem=in_send.at[k], recv_sem=in_recv.at[k],
            device_id=(j, z), device_id_type=MESH,
        )
        copy.start()
        sends.append(copy)
    own = pltpu.make_async_copy(x_ref.at[:, chunk(s)], recv.at[:, chunk(i)], own_sem)
    own.start()

    @pl.when(low_edge)
    def _():
        halo[:, 0] = jnp.zeros_like(halo[:, 0])

    @pl.when(high_edge)
    def _():
        halo[:, 1] = jnp.zeros_like(halo[:, 1])

    own.wait()
    for k in range(nl):
        j = (i + nl - k) % nl
        if k:
            sends[k - 1].wait_recv()
        block = lax.dot_general(
            recv[:, chunk(j)], win_ref[...], TN, preferred_element_type=jnp.float32,
        )
        carry[:, pl.ds(pl.multiple_of(j * w, w), w), :] = block.reshape(rows, w, ch)
    for copy in sends:
        copy.wait_send()

    def halo_copies(layer):
        up = pltpu.make_async_remote_copy(
            src_ref=edge.at[layer, 1], dst_ref=halo.at[layer, 0],
            send_sem=h_send.at[layer, 0], recv_sem=h_recv.at[layer, 0],
            device_id=(up_i, up_z), device_id_type=MESH,
        )
        down = pltpu.make_async_remote_copy(
            src_ref=edge.at[layer, 0], dst_ref=halo.at[layer, 1],
            send_sem=h_send.at[layer, 1], recv_sem=h_recv.at[layer, 1],
            device_id=(down_i, down_z), device_id_type=MESH,
        )
        return up, down

    def layer_step(step, _):
        layer = layers - 1 - step if backward else step
        d = dil[layer]

        def kernels():
            if backward:
                taps = [8 - (3 * b + a) for a in range(3) for b in range(3)]
            else:
                taps = [3 * b + a for a in range(3) for b in range(3)]
            return jnp.concatenate(
                [conv_ref[layer, tap] for tap in taps], axis=0 if backward else 1
            )

        def activity(r0, r1):
            a = carry[r0:r1]
            if backward:
                return a
            a = jnp.tanh(a)
            t_ref[layer, r0:r1] = (1.0 - a * a).astype(jnp.bfloat16)
            return a

        def widen(a, r0):
            n = a.shape[0]
            ext[r0:r0 + n, LON_PAD:LON_PAD + nlon, :] = a
            ext[r0:r0 + n, 0:LON_PAD, :] = a[:, nlon - LON_PAD:, :]
            ext[r0:r0 + n, LON_PAD + nlon:, :] = a[:, :LON_PAD, :]

        def columns(r0, r1):
            for b in range(3):
                cols[r0:r1, :, b * ch:(b + 1) * ch] = ext[
                    r0:r1, pl.ds(LON_PAD + (b - 1) * d, nlon), :
                ].astype(jnp.bfloat16)

        def convolved(r0, r1):
            n = r1 - r0
            windows = jnp.concatenate(
                [cols[pl.ds(DMAX + r0 + (a - 1) * d, n)].reshape(n * nlon, 3 * ch)
                 for a in range(3)], axis=1,
            )
            total = lax.dot_general(
                windows, kernels(), NN if backward else NT,
                preferred_element_type=jnp.float32,
            )
            total = total.reshape(n, nlon, ch)
            if backward:
                total = t_ref[layer, r0:r1].astype(jnp.float32) * total
            carry[r0:r1] = carry[r0:r1] + total

        low = activity(0, DMAX)
        high = activity(rows - DMAX, rows)
        edge[layer, 0] = low.astype(jnp.bfloat16)
        edge[layer, 1] = high.astype(jnp.bfloat16)
        up, down = halo_copies(layer)

        @pl.when(jnp.logical_not(high_edge))
        def _():
            up.start()

        @pl.when(jnp.logical_not(low_edge))
        def _():
            down.start()

        widen(low, DMAX)
        widen(high, rows)
        for r0 in range(DMAX, rows - DMAX, 8):
            widen(activity(r0, r0 + 8), DMAX + r0)
        for r0 in range(DMAX, DMAX + rows, 8):
            columns(r0, r0 + 8)
        for r0 in range(DMAX, rows - DMAX, 8):
            convolved(r0, r0 + 8)

        @pl.when(jnp.logical_not(high_edge))
        def _():
            up.wait_send()
            down.wait_recv()

        @pl.when(jnp.logical_not(low_edge))
        def _():
            down.wait_send()
            up.wait_recv()

        widen(halo[layer, 0].astype(jnp.float32), 0)
        widen(halo[layer, 1].astype(jnp.float32), DMAX + rows)
        columns(0, DMAX)
        columns(DMAX + rows, 2 * DMAX + rows)
        convolved(0, DMAX)
        convolved(rows - DMAX, rows)
        return 0

    lax.fori_loop(0, layers, layer_step, 0)

    def decode(j):
        block = carry[:, pl.ds(pl.multiple_of(j * w, w), w), :]
        outs[:, chunk(j)] = lax.dot_general(
            wout_ref[...], block.reshape(width, ch).astype(jnp.bfloat16), NT,
            preferred_element_type=jnp.float32,
        ).astype(jnp.bfloat16)

    sends = []
    for k in range(1, nl):
        j = (i + k) % nl
        decode(j)
        copy = pltpu.make_async_remote_copy(
            src_ref=outs.at[:, chunk(j)], dst_ref=land.at[:, chunk(s)],
            send_sem=o_send.at[k], recv_sem=o_recv.at[k],
            device_id=(j, z), device_id_type=MESH,
        )
        copy.start()
        sends.append(copy)
    decode(i)
    own = pltpu.make_async_copy(outs.at[:, chunk(i)], land.at[:, chunk(s)], own_sem)
    own.start()
    own.wait()
    for copy in sends:
        copy.wait()
    out_ref[...] = land[...]


def sweep(backward, nl, nz, dilations, x, w_in, conv, w_out, tanhs, rows, nlon):
    layers, ch = conv.shape[0], w_in.shape[1]
    vars_, cells = x.shape
    bf, f4 = jnp.bfloat16, jnp.float32
    vmem = pl.BlockSpec(memory_space=pltpu.VMEM)
    out_shape = [jax.ShapeDtypeStruct((vars_, cells), bf)]
    if not backward:
        out_shape.append(jax.ShapeDtypeStruct((layers, rows, nlon, ch), bf))
    args = [dilations, x, w_in, conv, w_out] + ([tanhs] if backward else [])
    dma = pltpu.SemaphoreType.DMA
    return pl.pallas_call(
        functools.partial(sweep_kernel, backward, nl, nz, layers),
        out_shape=out_shape,
        in_specs=[pl.BlockSpec(memory_space=pltpu.SMEM)] + [vmem] * (len(args) - 1),
        out_specs=[vmem] * len(out_shape),
        scratch_shapes=[
            pltpu.VMEM((rows, nlon, ch), f4),
            pltpu.VMEM((vars_, cells), bf),
            pltpu.VMEM((vars_, cells), bf),
            pltpu.VMEM((vars_, cells), bf),
            pltpu.VMEM((layers, 2, DMAX, nlon, ch), bf),
            pltpu.VMEM((layers, 2, DMAX, nlon, ch), bf),
            pltpu.VMEM((rows + 2 * DMAX, nlon + 2 * LON_PAD, ch), f4),
            pltpu.VMEM((rows + 2 * DMAX, nlon, 3 * ch), bf),
            dma((nl,)), dma((nl,)), dma((layers, 2)), dma((layers, 2)),
            dma((nl,)), dma((nl,)), dma(()),
        ],
        compiler_params=pltpu.CompilerParams(
            collective_id=1 if backward else 0, has_side_effects=True,
            vmem_limit_bytes=48 << 20,
        ),
    )(*args)


def on_device(background, encoder_weight, convolution_weight, decoder_weight, dilations,
              obs_values, obs_prec, obs_frac, obs_dest, obs_cell, obs_count):
    bf, f4 = jnp.bfloat16, jnp.float32
    nl, nz = lax.axis_size("lon"), lax.axis_size("lat")
    devices = nl * nz
    nvar, clon, clat = background.shape
    cells = clon * clat
    rows, nlon = clat // nl, clon * nl
    nrow = obs_dest.shape[0]
    capacity = 2 * nrow // devices
    total = 2 * nrow
    vpad = -(-nvar // 16) * 16

    target = obs_dest[:, 0]
    member = (target[:, None] == jnp.arange(devices, dtype=jnp.int32)[None, :]).astype(jnp.int32)
    before = jnp.sum((jnp.cumsum(member, axis=0) - member) * member, axis=1)
    slots = target * capacity + before
    alive = (jnp.arange(nrow, dtype=jnp.int32) < obs_count[0]).astype(f4)
    base = (obs_cell % (clat - 1)) * clon + obs_cell // (clat - 1)
    request = jnp.concatenate(
        [obs_values, (alive * obs_prec)[None], base.astype(f4)[None], obs_frac], axis=0
    )
    request = jnp.zeros((request.shape[0], total), f4).at[:, slots].set(request)
    arrived = lax.all_to_all(request, ("lon", "lat"), split_axis=1, concat_axis=1, tiled=True)
    owned_obs = arrived[:nvar]
    owned_prec = arrived[nvar]
    corner = arrived[nvar + 1].astype(jnp.int32)[:, None]
    u, v = arrived[nvar + 2][:, None], arrived[nvar + 3][:, None]
    place = lax.broadcasted_iota(jnp.int32, (total, cells), 1) - corner
    zero = jnp.zeros((), f4)
    values = jnp.where(place == clon, (1.0 - u) * v, jnp.where(place == clon + 1, u * v, zero))
    values = jnp.where(place == 1, u * (1.0 - v), values)
    values = jnp.where(place == 0, (1.0 - u) * (1.0 - v), values)
    stencil = lax.optimization_barrier(values.astype(bf))

    enc = jnp.pad(encoder_weight.T, ((0, vpad - nvar), (0, 0)))
    dec = jnp.pad(decoder_weight, ((0, vpad - nvar), (0, 0)))

    field0 = background.transpose(0, 2, 1).reshape(nvar, cells)
    field0 = jnp.pad(field0, ((0, vpad - nvar), (0, 0)))
    field = field0
    for iteration in range(ITERS):
        change, tanhs = sweep(
            False, nl, nz, dilations, field.astype(bf), enc, convolution_weight, dec, None, rows, nlon
        )
        forecast = field + change.astype(f4)
        head = forecast.astype(bf)
        tail = (forecast - head.astype(f4)).astype(bf)
        both = lax.dot_general(
            jnp.concatenate([head, tail], axis=0), stencil, NT, preferred_element_type=f4
        )
        equivalent = (both[:vpad] + both[vpad:])[:nvar]
        weighted = (owned_prec[None, :] * (equivalent - owned_obs)).astype(bf)
        weighted = jnp.pad(weighted, ((0, vpad - nvar), (0, 0)))
        grad = lax.dot_general(weighted, stencil, NN, preferred_element_type=f4)
        if iteration == ITERS - 1:
            returned = lax.all_to_all(
                equivalent.astype(bf), ("lon", "lat"), split_axis=1, concat_axis=1, tiled=True
            )
            innovation = alive[None, :] * (jnp.take(returned, slots, axis=1).astype(f4) - obs_values)
        back, = sweep(
            True, nl, nz, dilations, grad.astype(bf), dec, convolution_weight, enc, tanhs, rows, nlon
        )
        field = field - step_size * ((field - field0) + (grad + back.astype(f4)))
    analysis = field[:nvar].reshape(nvar, clat, clon).transpose(0, 2, 1)
    return analysis, innovation


def solution(mesh):
    placed = (
        P(None, "lon", "lat"), P(), P(), P(), P(),
        P(None, ("lon", "lat")), P(("lon", "lat")), P(None, ("lon", "lat")),
        P(("lon", "lat"), None), P(("lon", "lat")), P(("lon", "lat")),
    )
    return jax.shard_map(
        on_device, mesh=mesh, in_specs=placed,
        out_specs=(P(None, "lon", "lat"), P(None, ("lon", "lat"))), check_vma=False,
    )
```

```python
import functools

import jax
import jax.numpy as jnp
from jax import lax
from jax.experimental import pallas as pl
from jax.experimental.pallas import tpu as pltpu
from jax.sharding import PartitionSpec as P

DMAX = 4
ITERS = 2
step_size = 0.25
MESH = pl.DeviceIdType.MESH
NT = (((1,), (1,)), ((), ()))
TN = (((0,), (0,)), ((), ()))
NN = (((1,), (0,)), ((), ()))
LON_PAD = 8


def snake(i):
    return (i // 4) * 4 + ((i // 2 + i // 4) % 2) * 2 + i % 2


def flip(p, z, nl):
    return p + (z % 2) * (nl - 1 - 2 * p)


def sweep_kernel(backward, nl, nz, layers, dil, x_ref, win_ref, conv_ref, wout_ref, *refs):
    if backward:
        (t_ref, out_ref, carry, recv, outs, land, halo, edge, ext, cols,
         in_send, in_recv, h_send, h_recv, o_send, o_recv, own_sem) = refs
    else:
        (out_ref, t_ref, carry, recv, outs, land, halo, edge, ext, cols,
         in_send, in_recv, h_send, h_recv, o_send, o_recv, own_sem) = refs
    rows, nlon, ch = carry.shape
    w = nlon // nl
    width = rows * w
    i = lax.axis_index("lon")
    z = lax.axis_index("lat")
    s = flip(snake(i), z, nl)
    first = s == 0
    last = s == nl - 1
    low_edge = jnp.logical_and(first, z == 0)
    high_edge = jnp.logical_and(last, z == nz - 1)
    down_s = jnp.maximum(s - 1, 0)
    up_s = jnp.minimum(s + 1, nl - 1)
    down_i = jnp.where(first, i, snake(flip(down_s, z, nl)))
    up_i = jnp.where(last, i, snake(flip(up_s, z, nl)))
    down_z = jnp.where(first, jnp.maximum(z - 1, 0), z)
    up_z = jnp.where(last, jnp.minimum(z + 1, nz - 1), z)

    barrier = pltpu.get_barrier_semaphore()
    for k in range(1, nl):
        pl.semaphore_signal(barrier, inc=1, device_id=((i + k) % nl, z), device_id_type=MESH)

    @pl.when(jnp.logical_and(first, z > 0))
    def _():
        pl.semaphore_signal(barrier, inc=1, device_id=(i, down_z), device_id_type=MESH)

    @pl.when(jnp.logical_and(last, z < nz - 1))
    def _():
        pl.semaphore_signal(barrier, inc=1, device_id=(i, up_z), device_id_type=MESH)

    other_bands = (
        jnp.logical_and(first, z > 0).astype(jnp.int32)
        + jnp.logical_and(last, z < nz - 1).astype(jnp.int32)
    )
    pl.semaphore_wait(barrier, nl - 1 + other_bands)

    def chunk(number):
        return pl.ds(pl.multiple_of(number * width, width), width)

    sends = []
    for k in range(1, nl):
        j = (i + k) % nl
        copy = pltpu.make_async_remote_copy(
            src_ref=x_ref.at[:, chunk(flip(snake(j), z, nl))],
            dst_ref=recv.at[:, chunk(i)],
            send_sem=in_send.at[k], recv_sem=in_recv.at[k],
            device_id=(j, z), device_id_type=MESH,
        )
        copy.start()
        sends.append(copy)
    own = pltpu.make_async_copy(x_ref.at[:, chunk(s)], recv.at[:, chunk(i)], own_sem)
    own.start()

    @pl.when(low_edge)
    def _():
        halo[:, 0] = jnp.zeros_like(halo[:, 0])

    @pl.when(high_edge)
    def _():
        halo[:, 1] = jnp.zeros_like(halo[:, 1])

    own.wait()
    for k in range(nl):
        j = (i + nl - k) % nl
        if k:
            sends[k - 1].wait_recv()
        block = lax.dot_general(
            recv[:, chunk(j)], win_ref[...], TN, preferred_element_type=jnp.float32,
        )
        carry[:, pl.ds(pl.multiple_of(j * w, w), w), :] = block.reshape(rows, w, ch)
    for copy in sends:
        copy.wait_send()

    def halo_copies(layer):
        up = pltpu.make_async_remote_copy(
            src_ref=edge.at[layer, 1], dst_ref=halo.at[layer, 0],
            send_sem=h_send.at[layer, 0], recv_sem=h_recv.at[layer, 0],
            device_id=(up_i, up_z), device_id_type=MESH,
        )
        down = pltpu.make_async_remote_copy(
            src_ref=edge.at[layer, 0], dst_ref=halo.at[layer, 1],
            send_sem=h_send.at[layer, 1], recv_sem=h_recv.at[layer, 1],
            device_id=(down_i, down_z), device_id_type=MESH,
        )
        return up, down

    def layer_step(step, _):
        layer = layers - 1 - step if backward else step
        d = dil[layer]

        def kernels(a):
            if backward:
                taps = [8 - (3 * b + a) for b in range(3)]
            else:
                taps = [3 * b + a for b in range(3)]
            return jnp.concatenate(
                [conv_ref[layer, tap] for tap in taps], axis=0 if backward else 1
            )

        def activity(r0, r1):
            a = carry[r0:r1]
            if backward:
                return a
            a = jnp.tanh(a)
            t_ref[layer, r0:r1] = (1.0 - a * a).astype(jnp.bfloat16)
            return a

        def widen(a, r0):
            n = a.shape[0]
            ext[r0:r0 + n, LON_PAD:LON_PAD + nlon, :] = a
            ext[r0:r0 + n, 0:LON_PAD, :] = a[:, nlon - LON_PAD:, :]
            ext[r0:r0 + n, LON_PAD + nlon:, :] = a[:, :LON_PAD, :]

        def columns(r0, r1):
            for b in range(3):
                cols[r0:r1, :, b * ch:(b + 1) * ch] = ext[
                    r0:r1, pl.ds(LON_PAD + (b - 1) * d, nlon), :
                ].astype(jnp.bfloat16)

        def convolved(r0, r1):
            n = r1 - r0
            total = None
            for a in range(3):
                part = lax.dot_general(
                    cols[pl.ds(DMAX + r0 + (a - 1) * d, n)].reshape(n * nlon, 3 * ch),
                    kernels(a), NN if backward else NT,
                    preferred_element_type=jnp.float32,
                )
                total = part if total is None else total + part
            total = total.reshape(n, nlon, ch)
            if backward:
                total = t_ref[layer, r0:r1].astype(jnp.float32) * total
            carry[r0:r1] = carry[r0:r1] + total

        low = activity(0, DMAX)
        high = activity(rows - DMAX, rows)
        edge[layer, 0] = low.astype(jnp.bfloat16)
        edge[layer, 1] = high.astype(jnp.bfloat16)
        up, down = halo_copies(layer)

        @pl.when(jnp.logical_not(high_edge))
        def _():
            up.start()

        @pl.when(jnp.logical_not(low_edge))
        def _():
            down.start()

        widen(low, DMAX)
        widen(high, rows)
        for r0 in range(DMAX, rows - DMAX, 8):
            widen(activity(r0, r0 + 8), DMAX + r0)
        for r0 in range(DMAX, DMAX + rows, 8):
            columns(r0, r0 + 8)
        for r0 in range(DMAX, rows - DMAX, 8):
            convolved(r0, r0 + 8)

        @pl.when(jnp.logical_not(high_edge))
        def _():
            up.wait_send()
            down.wait_recv()

        @pl.when(jnp.logical_not(low_edge))
        def _():
            down.wait_send()
            up.wait_recv()

        widen(halo[layer, 0].astype(jnp.float32), 0)
        widen(halo[layer, 1].astype(jnp.float32), DMAX + rows)
        columns(0, DMAX)
        columns(DMAX + rows, 2 * DMAX + rows)
        convolved(0, DMAX)
        convolved(rows - DMAX, rows)
        return 0

    lax.fori_loop(0, layers, layer_step, 0)

    def decode(j):
        block = carry[:, pl.ds(pl.multiple_of(j * w, w), w), :]
        outs[:, chunk(j)] = lax.dot_general(
            wout_ref[...], block.reshape(width, ch).astype(jnp.bfloat16), NT,
            preferred_element_type=jnp.float32,
        ).astype(jnp.bfloat16)

    sends = []
    for k in range(1, nl):
        j = (i + k) % nl
        decode(j)
        copy = pltpu.make_async_remote_copy(
            src_ref=outs.at[:, chunk(j)], dst_ref=land.at[:, chunk(s)],
            send_sem=o_send.at[k], recv_sem=o_recv.at[k],
            device_id=(j, z), device_id_type=MESH,
        )
        copy.start()
        sends.append(copy)
    decode(i)
    own = pltpu.make_async_copy(outs.at[:, chunk(i)], land.at[:, chunk(s)], own_sem)
    own.start()
    own.wait()
    for copy in sends:
        copy.wait()
    out_ref[...] = land[...]


def sweep(backward, nl, nz, dilations, x, w_in, conv, w_out, tanhs, rows, nlon):
    layers, ch = conv.shape[0], w_in.shape[1]
    vars_, cells = x.shape
    bf, f4 = jnp.bfloat16, jnp.float32
    vmem = pl.BlockSpec(memory_space=pltpu.VMEM)
    out_shape = [jax.ShapeDtypeStruct((vars_, cells), bf)]
    if not backward:
        out_shape.append(jax.ShapeDtypeStruct((layers, rows, nlon, ch), bf))
    args = [dilations, x, w_in, conv, w_out] + ([tanhs] if backward else [])
    dma = pltpu.SemaphoreType.DMA
    return pl.pallas_call(
        functools.partial(sweep_kernel, backward, nl, nz, layers),
        out_shape=out_shape,
        in_specs=[pl.BlockSpec(memory_space=pltpu.SMEM)] + [vmem] * (len(args) - 1),
        out_specs=[vmem] * len(out_shape),
        scratch_shapes=[
            pltpu.VMEM((rows, nlon, ch), f4),
            pltpu.VMEM((vars_, cells), bf),
            pltpu.VMEM((vars_, cells), bf),
            pltpu.VMEM((vars_, cells), bf),
            pltpu.VMEM((layers, 2, DMAX, nlon, ch), bf),
            pltpu.VMEM((layers, 2, DMAX, nlon, ch), bf),
            pltpu.VMEM((rows + 2 * DMAX, nlon + 2 * LON_PAD, ch), f4),
            pltpu.VMEM((rows + 2 * DMAX, nlon, 3 * ch), bf),
            dma((nl,)), dma((nl,)), dma((layers, 2)), dma((layers, 2)),
            dma((nl,)), dma((nl,)), dma(()),
        ],
        compiler_params=pltpu.CompilerParams(
            collective_id=1 if backward else 0, has_side_effects=True,
            vmem_limit_bytes=48 << 20,
        ),
    )(*args)


def on_device(background, encoder_weight, convolution_weight, decoder_weight, dilations,
              obs_values, obs_prec, obs_frac, obs_dest, obs_cell, obs_count):
    bf, f4 = jnp.bfloat16, jnp.float32
    nl, nz = lax.axis_size("lon"), lax.axis_size("lat")
    devices = nl * nz
    nvar, clon, clat = background.shape
    cells = clon * clat
    rows, nlon = clat // nl, clon * nl
    nrow = obs_dest.shape[0]
    capacity = 2 * nrow // devices
    total = 2 * nrow
    vpad = -(-nvar // 16) * 16

    target = obs_dest[:, 0]
    member = (target[:, None] == jnp.arange(devices, dtype=jnp.int32)[None, :]).astype(jnp.int32)
    before = jnp.sum((jnp.cumsum(member, axis=0) - member) * member, axis=1)
    slots = target * capacity + before
    alive = (jnp.arange(nrow, dtype=jnp.int32) < obs_count[0]).astype(f4)
    base = (obs_cell % (clat - 1)) * clon + obs_cell // (clat - 1)
    request = jnp.concatenate(
        [obs_values, (alive * obs_prec)[None], base.astype(f4)[None], obs_frac], axis=0
    )
    request = jnp.zeros((request.shape[0], total), f4).at[:, slots].set(request)
    arrived = lax.all_to_all(request, ("lon", "lat"), split_axis=1, concat_axis=1, tiled=True)
    owned_obs = arrived[:nvar]
    owned_prec = arrived[nvar]
    corner = arrived[nvar + 1].astype(jnp.int32)[:, None]
    u, v = arrived[nvar + 2][:, None], arrived[nvar + 3][:, None]
    place = lax.broadcasted_iota(jnp.int32, (total, cells), 1) - corner
    zero = jnp.zeros((), f4)
    values = jnp.where(place == clon, (1.0 - u) * v, jnp.where(place == clon + 1, u * v, zero))
    values = jnp.where(place == 1, u * (1.0 - v), values)
    values = jnp.where(place == 0, (1.0 - u) * (1.0 - v), values)
    stencil = lax.optimization_barrier(values.astype(bf))

    enc = jnp.pad(encoder_weight.T, ((0, vpad - nvar), (0, 0)))
    dec = jnp.pad(decoder_weight, ((0, vpad - nvar), (0, 0)))

    field0 = background.transpose(0, 2, 1).reshape(nvar, cells)
    field0 = jnp.pad(field0, ((0, vpad - nvar), (0, 0)))
    field = field0
    for iteration in range(ITERS):
        change, tanhs = sweep(
            False, nl, nz, dilations, field.astype(bf), enc, convolution_weight, dec, None, rows, nlon
        )
        forecast = field + change.astype(f4)
        head = forecast.astype(bf)
        tail = (forecast - head.astype(f4)).astype(bf)
        both = lax.dot_general(
            jnp.concatenate([head, tail], axis=0), stencil, NT, preferred_element_type=f4
        )
        equivalent = (both[:vpad] + both[vpad:])[:nvar]
        weighted = (owned_prec[None, :] * (equivalent - owned_obs)).astype(bf)
        weighted = jnp.pad(weighted, ((0, vpad - nvar), (0, 0)))
        grad = lax.dot_general(weighted, stencil, NN, preferred_element_type=f4)
        if iteration == ITERS - 1:
            returned = lax.all_to_all(
                equivalent.astype(bf), ("lon", "lat"), split_axis=1, concat_axis=1, tiled=True
            )
            innovation = alive[None, :] * (jnp.take(returned, slots, axis=1).astype(f4) - obs_values)
        back, = sweep(
            True, nl, nz, dilations, grad.astype(bf), dec, convolution_weight, enc, tanhs, rows, nlon
        )
        field = field - step_size * ((field - field0) + (grad + back.astype(f4)))
    analysis = field[:nvar].reshape(nvar, clat, clon).transpose(0, 2, 1)
    return analysis, innovation


def solution(mesh):
    placed = (
        P(None, "lon", "lat"), P(), P(), P(), P(),
        P(None, ("lon", "lat")), P(("lon", "lat")), P(None, ("lon", "lat")),
        P(("lon", "lat"), None), P(("lon", "lat")), P(("lon", "lat")),
    )
    return jax.shard_map(
        on_device, mesh=mesh, in_specs=placed,
        out_specs=(P(None, "lon", "lat"), P(None, ("lon", "lat"))), check_vma=False,
    )
```
